32 devices in a mesh: dp: 8 (over y, x, core), tensor: 4 (over z).
Axes of the slice: x: 2, y: 2, z: 4, core: 2. Of those that a mesh axis runs over, the one named last changes fastest.
Arguments:
- latent_in: bfloat16 [16, 256, 768], P('dp', 'tensor'), may hold values from -6 to 6
- condition: bfloat16 [16, 768], P('dp'), may hold values from -6 to 6
- w_ada: bfloat16 [768, 4608], P('dp', 'tensor'), may hold values from -0.21875 to 0.21875
- w_qkv: bfloat16 [3, 768, 768], P(None, 'dp', 'tensor'), may hold values from -0.21875 to 0.21875
- w_proj: bfloat16 [768, 768], P('tensor', 'dp'), may hold values from -1.25 to 1.25
- w_up: bfloat16 [768, 3072], P('dp', 'tensor'), may hold values from -0.21875 to 0.21875
- w_down: bfloat16 [3072, 768], P('tensor', 'dp'), may hold values from -0.109375 to 0.109375
- out_grad: bfloat16 [16, 256, 768], P('dp', 'tensor'), may hold values from -6 to 6
Outputs:
- latent_out: bfloat16 [16, 256, 768], P('dp', 'tensor')
- grad_latent: float32 [16, 256, 768], P('dp', 'tensor')
- grad_condition: float32 [16, 768], P('dp')
- grad_ada: float32 [768, 4608], P('dp', 'tensor')
- grad_qkv: float32 [3, 768, 768], P(None, 'dp', 'tensor')
- grad_proj: float32 [768, 768], P('tensor', 'dp')
- grad_up: float32 [768, 3072], P('dp', 'tensor')
- grad_down: float32 [3072, 768], P('tensor', 'dp')
The draws below stay inside these ranges and needn't reach their ends.
All inputs are finite; a program needn't handle non-finite values.
Results may differ from the reference program's by a relative error of at most 0.015.
The reference program's roundings to bfloat16 on the way count: a program that leaves them out, or rounds other values in their place, can miss the bound.
Values may be sent and summed in bfloat16 or wider, within the bound.
A program may use at most 128 MiB of HBM per device.

```python
import math
import jax
import jax.numpy as jnp
from jax import lax

D = 768
HEADS = 12
HEAD_DIM = 64
FF = 3072
SEQ = 256
LATENTS = 16


def with_spikes(drawn, rng, source, target, parts, factor):
    def block_of(position):
        return (jnp.arange(drawn.shape[position]) // (drawn.shape[position] // parts)).reshape((-1,) + (1,) * (drawn.ndim - 1 - position))

    first = jax.random.permutation(rng, parts)[block_of(target)]
    far = (block_of(target) + parts // 2) % parts
    return jnp.where((block_of(source) == first) | (block_of(source) == far), factor * drawn, drawn)


def levels(rng, extent, pieces, low, top_value):
    level = 1.0
    for axis_at, parts in pieces:
        steps = jax.random.uniform(jax.random.fold_in(jax.random.fold_in(rng, 6), axis_at), (parts,), jnp.float32, low / len(pieces), top_value / len(pieces))
        level = level * jnp.repeat(jnp.exp(steps), extent[axis_at] // parts).reshape((-1,) + (1,) * (len(extent) - 1 - axis_at))
    return level


def noise(stream_key, extent, deviation, limit, split=(), dtype=jnp.bfloat16):
    array = jax.random.normal(stream_key, extent, jnp.float32) * deviation
    if len(split) > 0:
        array = levels(stream_key, extent, split, -0.22, 0.18) * array
    return jnp.clip(array, min=-limit, max=limit).astype(dtype)


def gaussian_with(key, extent, scale, reach, split, heavy, held_as=jnp.bfloat16):
    array = scale * jax.random.normal(key, extent, jnp.float32)
    if split:
        array = array * levels(key, extent, split, -0.22, 0.18)
    return jnp.clip(with_spikes(array, jax.random.fold_in(key, 3), *heavy), -reach, reach).astype(held_as)


def setup_inputs(seed: int = 0) -> dict:
    key_list = jax.random.split(jax.random.key(seed), 9)
    latent_in = noise(key_list[0], (LATENTS, SEQ, D), 1.0, 6.0, ((0, 8), (1, 4)))
    condition = noise(key_list[1], (LATENTS, D), 1.0, 6.0, ((0, 8),))
    w_ada = noise(key_list[2], (D, 6 * D), D ** -0.5, 0.21875, ((0, 8), (1, 4)))
    w_qkv = noise(key_list[3], (3, D, D), D ** -0.5, 0.21875, ((1, 8), (2, 4)))
    w_proj = noise(key_list[4], (D, D), (D // 32) ** -0.5, 1.25, ((0, 4), (1, 8)))
    w_up = noise(key_list[5], (D, FF), D ** -0.5, 0.21875, ((0, 8), (1, 4)))
    w_down = noise(key_list[6], (FF, D), FF ** -0.5, 0.109375, ((0, 4), (1, 8)))
    out_grad = gaussian_with(key_list[7], (LATENTS, SEQ, D), 1.0, 6.0, ((0, 8), (1, 4)), (0, 2, 8, 2.0))
    return {"latent_in": latent_in, "condition": condition, "w_ada": w_ada, "w_qkv": w_qkv, "w_proj": w_proj, "w_up": w_up, "w_down": w_down, "out_grad": out_grad}


@jax.custom_vjp
def low(v):
    return lax.optimization_barrier(v.astype(jnp.bfloat16)).astype(jnp.float32)

@jax.custom_vjp
def low_back(v):
    return v

def low_keep(v):
    return (low(v), None)

def low_pass(kept, grad):
    return (grad,)

def back_keep(v):
    return (v, None)

def back_low(kept, grad):
    return (low(grad),)
low.defvjp(low_keep, low_pass)
low_back.defvjp(back_keep, back_low)
epsilon = 1e-06

def silu_value(values):
    return values / (1.0 + jnp.exp(-values))

def gelu_tanh(values):
    return 0.5 * values * (1.0 + jnp.tanh(math.sqrt(2.0 / math.pi) * (values + 0.044715 * values * values * values)))

def normalize(values):
    centered = values - lax.optimization_barrier(jnp.mean(values, axis=-1, keepdims=True))
    variance = lax.optimization_barrier(jnp.mean(centered * centered, axis=-1, keepdims=True))
    return centered * lax.rsqrt(variance + epsilon)

def mix(form, left, right):
    return jnp.einsum(form, left, right, precision=lax.Precision.HIGHEST)

def block_forward(latent, condition, w_ada, w_qkv, w_proj, w_up, w_down):
    group = latent.shape[0]
    cond_act = low(silu_value(condition))
    modulation = low_back(mix('gd,de->ge', cond_act, w_ada)).reshape(group, 6, 1, D)
    shift_a = modulation[:, 0]
    scale_a = modulation[:, 1]
    gate_a = modulation[:, 2]
    shift_f = modulation[:, 3]
    scale_f = modulation[:, 4]
    gate_f = modulation[:, 5]
    normed_a = normalize(latent)
    attn_in = low(normed_a * (1.0 + scale_a) + shift_a)
    projected = low(low_back(mix('gsd,jde->jgse', attn_in, w_qkv)))
    projected = projected.reshape(3, group, SEQ, HEADS, HEAD_DIM)
    scores = low_back(mix('gqhe,gkhe->ghqk', projected[0], projected[1]) * HEAD_DIM ** (-0.5))
    shifted = jnp.exp(scores - lax.optimization_barrier(jnp.max(scores, axis=-1, keepdims=True)))
    soft_probs = shifted / lax.optimization_barrier(jnp.sum(shifted, axis=-1, keepdims=True))
    mixed = mix('ghqk,gkhe->gqhe', low(soft_probs), projected[2]).reshape(group, SEQ, D)
    mixed = low(low_back(mixed))
    attn_out = low_back(mix('gsd,de->gse', mixed, w_proj))
    resid = latent + gate_a * attn_out
    normed_f = normalize(resid)
    ffn_in = low(normed_f * (1.0 + scale_f) + shift_f)
    hidden_preactivation = low_back(mix('gsd,df->gsf', ffn_in, w_up))
    hidden_units = low(gelu_tanh(hidden_preactivation))
    ffn_out = low_back(mix('gsf,fd->gsd', hidden_units, w_down))
    return resid + gate_f * ffn_out

def reference(latent_in, condition, w_ada, w_qkv, w_proj, w_up, w_down, out_grad):
    weights = (w_ada.astype(jnp.float32), w_qkv.astype(jnp.float32), w_proj.astype(jnp.float32), w_up.astype(jnp.float32), w_down.astype(jnp.float32))
    group = math.gcd(LATENTS, 16)
    count = LATENTS // group
    latents = latent_in.astype(jnp.float32).reshape(count, group, SEQ, D)
    conditions = condition.astype(jnp.float32).reshape(count, group, D)
    cotangents = out_grad.astype(jnp.float32).reshape(count, group, SEQ, D)

    def step(carry, item):
        latent, cond_rows, cotangent = item
        result, pull = jax.vjp(block_forward, latent, cond_rows, *weights)
        grads = pull(cotangent)
        carry = tuple((total + part for total, part in zip(carry, grads[2:])))
        return (carry, (result.astype(jnp.bfloat16), grads[0], grads[1]))
    initial = tuple((jnp.zeros_like(weight) for weight in weights))
    totals, outputs = lax.scan(step, initial, (latents, conditions, cotangents))
    latent_out = outputs[0].reshape(LATENTS, SEQ, D)
    grad_latent = outputs[1].reshape(LATENTS, SEQ, D)
    grad_condition = outputs[2].reshape(LATENTS, D)
    return (latent_out, grad_latent, grad_condition, totals[0], totals[1], totals[2], totals[3], totals[4])
```

```python
import math

import jax
import jax.numpy as jnp
from jax import lax
from jax.sharding import PartitionSpec as P

HEAD_DIM = 64
EPS = 1e-06
f32 = jnp.float32
bf16 = jnp.bfloat16


def silu_value(values):
    return values / (1.0 + jnp.exp(-values))


def gelu_tanh(values):
    return (
        0.5
        * values
        * (
            1.0
            + jnp.tanh(math.sqrt(2.0 / math.pi) * (values + 0.044715 * values * values * values))
        )
    )


def norm_parts(values):
    centered = values - jnp.mean(values, axis=-1, keepdims=True)
    variance = jnp.mean(centered * centered, axis=-1, keepdims=True)
    inverse = lax.rsqrt(variance + EPS)
    return centered * inverse, inverse


def norm_back(normed, inverse, grad):
    return inverse * (
        grad
        - jnp.mean(grad, axis=-1, keepdims=True)
        - normed * jnp.mean(grad * normed, axis=-1, keepdims=True)
    )


def dot(form, left, right):
    return jnp.einsum(form, left, right, preferred_element_type=f32)


def gather_tensor(block, axis):
    return lax.all_gather(block, "tensor", axis=axis, tiled=True)


def reduce_tensor(part):
    return lax.psum(part.astype(bf16), "tensor").astype(f32)


def scatter_tensor(part):
    return lax.psum_scatter(
        part.astype(bf16), "tensor", scatter_dimension=1, tiled=True
    ).astype(f32)


def gather_weights(shard):
    return lax.all_gather(shard, "dp", axis=0, tiled=True)


def scatter_grads(grads):
    return lax.psum_scatter(grads.astype(bf16), "dp", scatter_dimension=0, tiled=True).astype(f32)


def modulation_of(cond_mine, w_ada):
    part = jnp.dot(cond_mine, w_ada, preferred_element_type=f32)
    own = lax.psum_scatter(part, "dp", scatter_dimension=0, tiled=True)
    return lax.all_gather(own, "tensor", axis=1, tiled=True)


def shards(latent_in, condition, w_ada, w_qkv, w_proj, w_up, w_down, out_grad):
    rows, own_tokens, width = latent_in.shape
    scale = HEAD_DIM ** (-0.5)
    dp_at = lax.axis_index("dp")
    tensor_at = lax.axis_index("tensor")
    shard_rows = w_ada.shape[0]
    local = w_proj.shape[0]
    heads = local // HEAD_DIM
    units = w_down.shape[0]

    attn_shard = jnp.concatenate(
        [w_qkv[0], w_qkv[1], w_qkv[2], w_proj.T], axis=1
    )
    ffn_shard = jnp.concatenate([w_up, w_down.T], axis=1)
    cond_all = lax.all_gather(condition, "dp", axis=0, tiled=True)
    cond_act = silu_value(cond_all.astype(f32)).astype(bf16)
    cond_mine = lax.dynamic_slice_in_dim(cond_act, dp_at * shard_rows, shard_rows, 1)
    modulation = modulation_of(cond_mine, w_ada).reshape(rows, 6, 1, width)
    shift_a, scale_a, gate_a, shift_f, scale_f, gate_f = (modulation[:, i] for i in range(6))

    attn_weights = gather_weights(attn_shard)
    w_in = attn_weights[:, : 3 * local]
    proj_t = attn_weights[:, 3 * local :]
    both = gather_tensor(jnp.stack([latent_in, out_grad], axis=0), 2)
    ffn_weights = gather_weights(ffn_shard)
    up = ffn_weights[:, :units]
    down_t = ffn_weights[:, units:]

    tokens = both[0].astype(f32)
    cotangent = both[1].astype(f32)
    seq = tokens.shape[1]

    normed_a, inverse_a = norm_parts(tokens)
    attn_in = (normed_a * (1.0 + scale_a) + shift_a).astype(bf16)
    projected = dot("lsd,de->lse", attn_in, w_in).astype(bf16)
    projected = projected.reshape(rows, seq, 3, heads, HEAD_DIM)
    queries, keys, values = projected[:, :, 0], projected[:, :, 1], projected[:, :, 2]
    scores = dot("lqhe,lkhe->lhqk", queries, keys) * scale
    shifted = jnp.exp(scores - jnp.max(scores, axis=-1, keepdims=True))
    probs = shifted / jnp.sum(shifted, axis=-1, keepdims=True)
    probs_low = probs.astype(bf16)
    mixed = dot("lhqk,lkhe->lqhe", probs_low, values).reshape(rows, seq, local).astype(bf16)
    attn_out = reduce_tensor(dot("lsd,ed->lse", mixed, proj_t))
    resid = tokens + gate_a * attn_out
    normed_f, inverse_f = norm_parts(resid)
    ffn_in = (normed_f * (1.0 + scale_f) + shift_f).astype(bf16)
    hidden_pre = dot("lsd,dn->lsn", ffn_in, up)
    hidden, gelu_pull = jax.vjp(gelu_tanh, hidden_pre)
    hidden = hidden.astype(bf16)
    d_ffn_out = (gate_f * cotangent).astype(bf16)
    d_hidden_pre = gelu_pull(dot("lse,en->lsn", d_ffn_out, down_t))[0].astype(bf16)
    d_ffn_in = reduce_tensor(dot("lsn,dn->lsd", d_hidden_pre, up))

    ffn_part = dot("lsn,en->lse", hidden, down_t)
    d_gate_f = jnp.sum(cotangent * ffn_part, axis=1)
    ffn_own = scatter_tensor(ffn_part)
    first = tensor_at * own_tokens
    resid_own = lax.dynamic_slice_in_dim(resid, first, own_tokens, 1)
    latent_out = (resid_own + gate_f * ffn_own).astype(bf16)

    grad_ffn = jnp.concatenate(
        [dot("lsd,lsn->dn", ffn_in, d_hidden_pre), dot("lse,lsn->en", d_ffn_out, hidden)], axis=1
    )
    grad_ffn = scatter_grads(grad_ffn)

    d_shift_f = jnp.sum(d_ffn_in, axis=1)
    d_scale_f = jnp.sum(d_ffn_in * normed_f, axis=1)
    d_resid = cotangent + norm_back(normed_f, inverse_f, d_ffn_in * (1.0 + scale_f))
    d_gate_a = jnp.sum(d_resid * attn_out, axis=1)
    d_attn_out = (gate_a * d_resid).astype(bf16)
    d_mixed = dot("lse,ed->lsd", d_attn_out, proj_t).astype(bf16)
    d_mixed = d_mixed.reshape(rows, seq, heads, HEAD_DIM)
    d_probs = dot("lqhe,lkhe->lhqk", d_mixed, values)
    d_scores = probs * (d_probs - jnp.sum(d_probs * probs, axis=-1, keepdims=True))
    d_scores = d_scores.astype(bf16)
    d_values = dot("lhqk,lqhe->lkhe", probs_low, d_mixed)
    d_queries = dot("lhqk,lkhe->lqhe", d_scores, keys) * scale
    d_keys = dot("lhqk,lqhe->lkhe", d_scores, queries) * scale
    d_projected = jnp.stack([d_queries, d_keys, d_values], axis=2)
    d_projected = d_projected.reshape(rows, seq, 3 * local).astype(bf16)
    d_attn_part = dot("lse,de->lsd", d_projected, w_in)

    d_attn_own = scatter_tensor(d_attn_part)
    grad_attn = jnp.concatenate(
        [dot("lsd,lse->de", attn_in, d_projected), dot("lse,lsd->ed", d_attn_out, mixed)], axis=1
    )
    grad_attn = scatter_grads(grad_attn)

    own = lambda value: lax.dynamic_slice_in_dim(value, first, own_tokens, 1)
    grad_latent = own(d_resid) + norm_back(
        own(normed_a), own(inverse_a), d_attn_own * (1.0 + scale_a)
    )

    d_shift_a = jnp.sum(d_attn_part, axis=1)
    d_scale_a = jnp.sum(d_attn_part * normed_a, axis=1)
    ones = jnp.where(tensor_at == 0, 1.0, 0.0)
    d_modulation = jnp.concatenate(
        [d_shift_a, d_scale_a, d_gate_a * ones, d_shift_f * ones, d_scale_f * ones, d_gate_f],
        axis=1,
    )
    d_mod_own = lax.psum_scatter(d_modulation, "tensor", scatter_dimension=1, tiled=True)
    d_mod_all = lax.all_gather(d_mod_own.astype(bf16), "dp", axis=0, tiled=True)
    grad_ada = dot("ld,le->de", cond_mine, d_mod_all)
    act_part = dot("le,de->ld", d_mod_all, w_ada)
    act_all = lax.all_gather(act_part, ("dp", "tensor"), axis=0, tiled=False)
    act_all = act_all.reshape(-1, lax.axis_size("tensor"), cond_all.shape[0], shard_rows)
    act_own = lax.dynamic_slice_in_dim(act_all, dp_at * rows, rows, 2)
    d_act = jnp.sum(act_own, axis=1).transpose(1, 0, 2).reshape(rows, width)
    grad_condition = jax.vjp(silu_value, condition.astype(f32))[1](d_act)[0]

    grad_qkv = jnp.stack([grad_attn[:, j * local : (j + 1) * local] for j in range(3)], axis=0)
    grad_proj = grad_attn[:, 3 * local :].T
    grad_up = grad_ffn[:, :units]
    grad_down = grad_ffn[:, units:].T
    return (
        latent_out,
        grad_latent,
        grad_condition,
        grad_ada,
        grad_qkv,
        grad_proj,
        grad_up,
        grad_down,
    )


def solution(mesh):
    return jax.shard_map(
        shards,
        mesh=mesh,
        in_specs=(
            P("dp", "tensor", None),
            P("dp", None),
            P("dp", "tensor"),
            P(None, "dp", "tensor"),
            P("tensor", "dp"),
            P("dp", "tensor"),
            P("tensor", "dp"),
            P("dp", "tensor", None),
        ),
        out_specs=(
            P("dp", "tensor", None),
            P("dp", "tensor", None),
            P("dp", None),
            P("dp", "tensor"),
            P(None, "dp", "tensor"),
            P("tensor", "dp"),
            P("dp", "tensor"),
            P("tensor", "dp"),
        ),
        check_vma=False,
    )
```

```python
import math

import jax
import jax.numpy as jnp
from jax import lax
from jax.experimental import pallas as pl
from jax.experimental.pallas import tpu as pltpu
from jax.sharding import PartitionSpec as P

MESH = pl.DeviceIdType.MESH
VMEM = pl.BlockSpec(memory_space=pltpu.VMEM)

HEAD_DIM = 64
EPS = 1e-06
f32 = jnp.float32
bf16 = jnp.bfloat16


def silu_value(values):
    return values / (1.0 + jnp.exp(-values))


def gelu_tanh(values):
    return (
        0.5
        * values
        * (
            1.0
            + jnp.tanh(math.sqrt(2.0 / math.pi) * (values + 0.044715 * values * values * values))
        )
    )


def norm_parts(values):
    centered = values - jnp.mean(values, axis=-1, keepdims=True)
    variance = jnp.mean(centered * centered, axis=-1, keepdims=True)
    inverse = lax.rsqrt(variance + EPS)
    return centered * inverse, inverse


def norm_back(normed, inverse, grad):
    return inverse * (
        grad
        - jnp.mean(grad, axis=-1, keepdims=True)
        - normed * jnp.mean(grad * normed, axis=-1, keepdims=True)
    )


def dot(form, left, right):
    return jnp.einsum(form, left, right, preferred_element_type=f32)


def gather_tensor(block, axis):
    return lax.all_gather(block, "tensor", axis=axis, tiled=True)


def gather_weights(shard):
    return lax.all_gather(shard, "dp", axis=0, tiled=True)


def greet(axes):
    barrier = pltpu.get_barrier_semaphore()
    total = 0
    for axis in axes:
        size = lax.axis_size(axis)
        me = lax.axis_index(axis)
        for step in range(1, size):
            pl.semaphore_signal(
                barrier, inc=1, device_id={axis: lax.rem(me + step, size)}, device_id_type=MESH
            )
        total += size - 1
    pl.semaphore_wait(barrier, total)


def start_exchange(axis, source, target, sems):
    size = lax.axis_size(axis)
    me = lax.axis_index(axis)
    copies = []
    for step in range(1, size):
        peer = lax.rem(me + step, size)
        copy = pltpu.make_async_remote_copy(
            src_ref=source(peer),
            dst_ref=target,
            send_sem=sems.at[0, step - 1],
            recv_sem=sems.at[1, step - 1],
            device_id={axis: peer},
            device_id_type=MESH,
        )
        copy.start()
        copies.append(copy)
    return copies


def wait_all(copies):
    for copy in copies:
        copy.wait()


def exchange(axis, source, target, sems):
    wait_all(start_exchange(axis, source, target, sems))


def sem_pair(axis):
    return pltpu.SemaphoreType.DMA((2, lax.axis_size(axis) - 1))


def call(kernel, outs, scratch, number, *args):
    return pl.pallas_call(
        kernel,
        out_shape=outs,
        in_specs=[VMEM] * len(args),
        out_specs=jax.tree.map(lambda _: VMEM, outs),
        scratch_shapes=scratch,
        compiler_params=pltpu.CompilerParams(
            collective_id=number, has_side_effects=True, vmem_limit_bytes=48 * 2**20
        ),
    )(*args)


def modulation_kernel(cond_ref, w_ref, mod_ref, act_ref, cond_buf, part, recv, own, s0, s1, s2):
    count = lax.axis_size("dp")
    me, mine = lax.axis_index("dp"), lax.axis_index("tensor")
    greet(("dp", "tensor"))
    copies = start_exchange("dp", lambda peer: cond_ref.at[peer], cond_buf.at[me], s0)
    cond_buf[me] = cond_ref[me]
    wait_all(copies)

    @pl.loop(0, count)
    def _(at):
        act = silu_value(cond_buf[at]).astype(bf16)
        act_ref[at] = act.astype(f32)
        part[at] = jnp.dot(act, w_ref[...], preferred_element_type=f32)

    copies = start_exchange("dp", lambda peer: part.at[peer], recv.at[me], s1)
    recv[me] = part[me]
    wait_all(copies)
    own[...] = jnp.sum(recv[...], axis=0)
    copies = start_exchange("tensor", lambda peer: own, mod_ref.at[mine], s2)
    mod_ref[mine] = own[...]
    wait_all(copies)


def modulation_of(condition, w_ada):
    count, group = lax.axis_size("dp"), lax.axis_size("tensor")
    rows, width = condition.shape
    shard_rows, columns = w_ada.shape
    blocks = condition.astype(f32).reshape(rows, count, shard_rows).transpose(1, 0, 2)
    mod, act = call(
        modulation_kernel,
        (
            jax.ShapeDtypeStruct((group, rows, columns), f32),
            jax.ShapeDtypeStruct((count, rows, shard_rows), f32),
        ),
        [
            pltpu.VMEM((count, rows, shard_rows), f32),
            pltpu.VMEM((count, rows, columns), f32),
            pltpu.VMEM((count, rows, columns), f32),
            pltpu.VMEM((rows, columns), f32),
            sem_pair("dp"),
            sem_pair("dp"),
            sem_pair("tensor"),
        ],
        1,
        blocks,
        w_ada,
    )
    mod = mod.transpose(1, 0, 2).reshape(rows, group * columns)
    return mod, act.reshape(count * rows, shard_rows).astype(bf16)


def condition_kernel(
    part_ref, w_ref, all_ref, act_ref, recv, own, part, terms, gathered, s0, s1, s2, s3
):
    count = lax.axis_size("dp")
    me, mine = lax.axis_index("dp"), lax.axis_index("tensor")
    greet(("dp", "tensor"))
    copies = start_exchange("tensor", lambda peer: part_ref.at[peer], recv.at[mine], s0)
    recv[mine] = part_ref[mine]
    wait_all(copies)
    own[...] = jnp.sum(recv[...], axis=0).astype(bf16).astype(f32)
    copies = start_exchange("dp", lambda peer: own, all_ref.at[me], s1)
    all_ref[me] = own[...]
    wait_all(copies)

    @pl.loop(0, count)
    def _(at):
        part[at] = lax.dot_general(
            all_ref[at].astype(bf16),
            w_ref[...],
            (((1,), (1,)), ((), ())),
            preferred_element_type=f32,
        )

    copies = start_exchange("dp", lambda peer: part.at[peer], terms.at[me], s2)
    terms[me] = part[me]
    wait_all(copies)
    copies = start_exchange("tensor", lambda peer: terms, gathered.at[mine], s3)
    gathered[mine] = terms[...]
    wait_all(copies)
    act_ref[...] = jnp.sum(gathered[...], axis=0)


def condition_back(parts, w_ada):
    count, group = lax.axis_size("dp"), lax.axis_size("tensor")
    rows = parts.shape[0]
    shard_rows, columns = w_ada.shape
    blocks = parts.reshape(rows, group, columns).transpose(1, 0, 2)
    everyone, act = call(
        condition_kernel,
        (
            jax.ShapeDtypeStruct((count, rows, columns), f32),
            jax.ShapeDtypeStruct((count, rows, shard_rows), f32),
        ),
        [
            pltpu.VMEM((group, rows, columns), f32),
            pltpu.VMEM((rows, columns), f32),
            pltpu.VMEM((count, rows, shard_rows), f32),
            pltpu.VMEM((count, rows, shard_rows), f32),
            pltpu.VMEM((group, count, rows, shard_rows), f32),
            sem_pair("tensor"),
            sem_pair("dp"),
            sem_pair("dp"),
            sem_pair("tensor"),
        ],
        2,
        blocks,
        w_ada,
    )
    everyone = everyone.reshape(count * rows, columns).astype(bf16)
    return everyone, act.transpose(1, 0, 2).reshape(rows, count * shard_rows)


def token_block(ref, at, size):
    return ref.at[:, pl.ds(pl.multiple_of(at * size, size), size)]


def reduce_kernel(part_ref, out_ref, recv, s0, s1):
    group = lax.axis_size("tensor")
    mine = lax.axis_index("tensor")
    size = part_ref.shape[1] // group
    greet(("tensor",))
    exchange("tensor", lambda peer: token_block(part_ref, peer, size), recv.at[mine], s0)
    total = token_block(part_ref, mine, size)[...].astype(f32)
    for step in range(1, group):
        total += recv[lax.rem(mine + step, group)].astype(f32)
    own = token_block(out_ref, mine, size)
    own[...] = total.astype(bf16)
    exchange("tensor", lambda peer: own, own, s1)


def reduce_tensor(part, number):
    group = lax.axis_size("tensor")
    rows, seq, width = part.shape
    return call(
        reduce_kernel,
        jax.ShapeDtypeStruct(part.shape, bf16),
        [
            pltpu.VMEM((group, rows, seq // group, width), bf16),
            sem_pair("tensor"),
            sem_pair("tensor"),
        ],
        number,
        part.astype(bf16),
    ).astype(f32)


def final_kernel(
    attn_ref, ffn_ref, grad_ref, attn_out, ffn_out, grad_out, attn_recv, ffn_recv, pair_recv,
    stage, grad_recv, s0, s1, s2, s3
):
    group = lax.axis_size("tensor")
    count = lax.axis_size("dp")
    pairs = count // 2
    me, mine = lax.axis_index("dp"), lax.axis_index("tensor")
    chip, side = me // 2, lax.rem(me, 2)
    size = attn_ref.shape[1] // group
    greet(("dp", "tensor"))
    pair_copy = pltpu.make_async_remote_copy(
        src_ref=grad_ref.at[:, 1 - side],
        dst_ref=pair_recv,
        send_sem=s0.at[0],
        recv_sem=s0.at[1],
        device_id={"dp": 2 * chip + 1 - side},
        device_id_type=MESH,
    )
    pair_copy.start()
    attn_copies = start_exchange(
        "tensor", lambda peer: token_block(attn_ref, peer, size), attn_recv.at[mine], s1
    )
    ffn_copies = start_exchange(
        "tensor", lambda peer: token_block(ffn_ref, peer, size), ffn_recv.at[mine], s2
    )
    pair_copy.wait()
    grad_copies = []
    for step in range(pairs):
        to = lax.rem(chip + step, pairs) if step else chip
        total = grad_ref[to, side].astype(f32) + pair_recv[to].astype(f32)
        if step == 0:
            grad_out[...] = total
            continue
        stage[to] = total.astype(bf16)
        copy = pltpu.make_async_remote_copy(
            src_ref=stage.at[to],
            dst_ref=grad_recv.at[chip],
            send_sem=s3.at[0, step - 1],
            recv_sem=s3.at[1, step - 1],
            device_id={"dp": 2 * to + side},
            device_id_type=MESH,
        )
        copy.start()
        grad_copies.append(copy)
    wait_all(grad_copies)
    for step in range(1, pairs):
        grad_out[...] += grad_recv[lax.rem(chip + step, pairs)].astype(f32)
    for copies, source, recv, out in (
        (attn_copies, attn_ref, attn_recv, attn_out),
        (ffn_copies, ffn_ref, ffn_recv, ffn_out),
    ):
        wait_all(copies)
        total = token_block(source, mine, size)[...].astype(f32)
        for step in range(1, group):
            total += recv[lax.rem(mine + step, group)].astype(f32)
        out[...] = total


def final_sums(attn_part, ffn_part, grads):
    group, count = lax.axis_size("tensor"), lax.axis_size("dp")
    rows, seq, width = attn_part.shape
    depth, columns = grads.shape
    shard_rows = depth // count
    tokens = (rows, seq // group, width)
    return call(
        final_kernel,
        (
            jax.ShapeDtypeStruct(tokens, f32),
            jax.ShapeDtypeStruct(tokens, f32),
            jax.ShapeDtypeStruct((shard_rows, columns), f32),
        ),
        [
            pltpu.VMEM((group,) + tokens, bf16),
            pltpu.VMEM((group,) + tokens, bf16),
            pltpu.VMEM((count // 2, shard_rows, columns), bf16),
            pltpu.VMEM((count // 2, shard_rows, columns), bf16),
            pltpu.VMEM((count // 2, shard_rows, columns), bf16),
            pltpu.SemaphoreType.DMA((2,)),
            sem_pair("tensor"),
            sem_pair("tensor"),
            pltpu.SemaphoreType.DMA((2, count // 2 - 1)),
        ],
        5,
        attn_part.astype(bf16),
        ffn_part.astype(bf16),
        grads.astype(bf16).reshape(count // 2, 2, shard_rows, columns),
    )


def shards(latent_in, condition, w_ada, w_qkv, w_proj, w_up, w_down, out_grad):
    rows, own_tokens, width = latent_in.shape
    scale = HEAD_DIM ** (-0.5)
    tensor_at = lax.axis_index("tensor")
    local = w_proj.shape[0]
    heads = local // HEAD_DIM
    units = w_down.shape[0]

    attn_shard = jnp.concatenate(
        [w_qkv[0], w_qkv[1], w_qkv[2], w_proj.T], axis=1
    )
    ffn_shard = jnp.concatenate([w_up, w_down.T], axis=1)
    modulation, cond_mine = modulation_of(condition, w_ada)
    modulation = modulation.reshape(rows, 6, 1, width)
    shift_a, scale_a, gate_a, shift_f, scale_f, gate_f = (modulation[:, i] for i in range(6))

    attn_weights = gather_weights(attn_shard)
    w_in = attn_weights[:, : 3 * local]
    proj_t = attn_weights[:, 3 * local :]
    both = gather_tensor(jnp.stack([latent_in, out_grad], axis=0), 2)
    ffn_weights = gather_weights(ffn_shard)
    up = ffn_weights[:, :units]
    down_t = ffn_weights[:, units:]

    tokens = both[0].astype(f32)
    cotangent = both[1].astype(f32)
    seq = tokens.shape[1]

    normed_a, inverse_a = norm_parts(tokens)
    attn_in = (normed_a * (1.0 + scale_a) + shift_a).astype(bf16)
    projected = dot("lsd,de->lse", attn_in, w_in).astype(bf16)
    projected = projected.reshape(rows, seq, 3, heads, HEAD_DIM)
    queries, keys, values = projected[:, :, 0], projected[:, :, 1], projected[:, :, 2]
    scores = dot("lqhe,lkhe->lhqk", queries, keys) * scale
    shifted = jnp.exp(scores - jnp.max(scores, axis=-1, keepdims=True))
    probs = shifted / jnp.sum(shifted, axis=-1, keepdims=True)
    probs_low = probs.astype(bf16)
    mixed = dot("lhqk,lkhe->lqhe", probs_low, values).reshape(rows, seq, local).astype(bf16)
    attn_out = reduce_tensor(dot("lsd,ed->lse", mixed, proj_t), 3)
    resid = tokens + gate_a * attn_out
    normed_f, inverse_f = norm_parts(resid)
    ffn_in = (normed_f * (1.0 + scale_f) + shift_f).astype(bf16)
    hidden_pre = dot("lsd,dn->lsn", ffn_in, up)
    hidden, gelu_pull = jax.vjp(gelu_tanh, hidden_pre)
    hidden = hidden.astype(bf16)
    d_ffn_out = (gate_f * cotangent).astype(bf16)
    d_hidden_pre = gelu_pull(dot("lse,en->lsn", d_ffn_out, down_t))[0].astype(bf16)
    d_ffn_in = reduce_tensor(dot("lsn,dn->lsd", d_hidden_pre, up), 4)

    ffn_part = dot("lsn,en->lse", hidden, down_t)
    d_gate_f = jnp.sum(cotangent * ffn_part, axis=1)
    d_shift_f = jnp.sum(d_ffn_in, axis=1)
    d_scale_f = jnp.sum(d_ffn_in * normed_f, axis=1)
    d_resid = cotangent + norm_back(normed_f, inverse_f, d_ffn_in * (1.0 + scale_f))
    d_gate_a = jnp.sum(d_resid * attn_out, axis=1)
    d_attn_out = (gate_a * d_resid).astype(bf16)
    d_mixed = dot("lse,ed->lsd", d_attn_out, proj_t).astype(bf16)
    d_mixed = d_mixed.reshape(rows, seq, heads, HEAD_DIM)
    d_probs = dot("lqhe,lkhe->lhqk", d_mixed, values)
    d_scores = probs * (d_probs - jnp.sum(d_probs * probs, axis=-1, keepdims=True))
    d_scores = d_scores.astype(bf16)
    d_values = dot("lhqk,lqhe->lkhe", probs_low, d_mixed)
    d_queries = dot("lhqk,lkhe->lqhe", d_scores, keys) * scale
    d_keys = dot("lhqk,lqhe->lkhe", d_scores, queries) * scale
    d_projected = jnp.stack([d_queries, d_keys, d_values], axis=2)
    d_projected = d_projected.reshape(rows, seq, 3 * local).astype(bf16)
    d_attn_part = dot("lse,de->lsd", d_projected, w_in)

    grads = jnp.concatenate(
        [
            dot("lsd,lse->de", attn_in, d_projected).astype(bf16),
            dot("lse,lsd->ed", d_attn_out, mixed).astype(bf16),
            dot("lsd,lsn->dn", ffn_in, d_hidden_pre).astype(bf16),
            dot("lse,lsn->en", d_ffn_out, hidden).astype(bf16),
        ],
        axis=1,
    )
    d_attn_own, ffn_own, grads = final_sums(d_attn_part, ffn_part, grads)
    grad_attn, grad_ffn = grads[:, : 4 * local], grads[:, 4 * local :]
    first = tensor_at * own_tokens
    own = lambda value: lax.dynamic_slice_in_dim(value, first, own_tokens, 1)
    latent_out = (own(resid) + gate_f * ffn_own).astype(bf16)
    grad_latent = own(d_resid) + norm_back(
        own(normed_a), own(inverse_a), d_attn_own * (1.0 + scale_a)
    )

    d_shift_a = jnp.sum(d_attn_part, axis=1)
    d_scale_a = jnp.sum(d_attn_part * normed_a, axis=1)
    ones = jnp.where(tensor_at == 0, 1.0, 0.0)
    d_modulation = jnp.concatenate(
        [d_shift_a, d_scale_a, d_gate_a * ones, d_shift_f * ones, d_scale_f * ones, d_gate_f],
        axis=1,
    )
    d_mod_all, d_act = condition_back(d_modulation, w_ada)
    grad_ada = dot("ld,le->de", cond_mine, d_mod_all)
    grad_condition = jax.vjp(silu_value, condition.astype(f32))[1](d_act)[0]

    grad_qkv = jnp.stack([grad_attn[:, j * local : (j + 1) * local] for j in range(3)], axis=0)
    grad_proj = grad_attn[:, 3 * local :].T
    grad_up = grad_ffn[:, :units]
    grad_down = grad_ffn[:, units:].T
    return (
        latent_out,
        grad_latent,
        grad_condition,
        grad_ada,
        grad_qkv,
        grad_proj,
        grad_up,
        grad_down,
    )


def solution(mesh):
    return jax.shard_map(
        shards,
        mesh=mesh,
        in_specs=(
            P("dp", "tensor", None),
            P("dp", None),
            P("dp", "tensor"),
            P(None, "dp", "tensor"),
            P("tensor", "dp"),
            P("dp", "tensor"),
            P("tensor", "dp"),
            P("dp", "tensor", None),
        ),
        out_specs=(
            P("dp", "tensor", None),
            P("dp", "tensor", None),
            P("dp", None),
            P("dp", "tensor"),
            P(None, "dp", "tensor"),
            P("tensor", "dp"),
            P("dp", "tensor"),
            P("tensor", "dp"),
        ),
        check_vma=False,
    )
```

```python
import math

import jax
import jax.numpy as jnp
from jax import lax
from jax.experimental import pallas as pl
from jax.experimental.pallas import tpu as pltpu
from jax.sharding import PartitionSpec as P

MESH = pl.DeviceIdType.MESH
VMEM = pl.BlockSpec(memory_space=pltpu.VMEM)

HEAD_DIM = 64
EPS = 1e-06
f32 = jnp.float32
bf16 = jnp.bfloat16


def silu_value(values):
    return values / (1.0 + jnp.exp(-values))


def gelu_tanh(values):
    return (
        0.5
        * values
        * (
            1.0
            + jnp.tanh(math.sqrt(2.0 / math.pi) * (values + 0.044715 * values * values * values))
        )
    )


def norm_parts(values):
    centered = values - jnp.mean(values, axis=-1, keepdims=True)
    variance = jnp.mean(centered * centered, axis=-1, keepdims=True)
    inverse = lax.rsqrt(variance + EPS)
    return centered * inverse, inverse


def norm_back(normed, inverse, grad):
    return inverse * (
        grad
        - jnp.mean(grad, axis=-1, keepdims=True)
        - normed * jnp.mean(grad * normed, axis=-1, keepdims=True)
    )


def dot(form, left, right):
    return jnp.einsum(form, left, right, preferred_element_type=f32)


def gather_tensor(block, axis):
    return lax.all_gather(block, "tensor", axis=axis, tiled=True)


def gather_weights(shard):
    return lax.all_gather(shard, "dp", axis=0, tiled=True)


def greet(axes):
    barrier = pltpu.get_barrier_semaphore()
    total = 0
    for axis in axes:
        size = lax.axis_size(axis)
        me = lax.axis_index(axis)
        for step in range(1, size):
            pl.semaphore_signal(
                barrier, inc=1, device_id={axis: lax.rem(me + step, size)}, device_id_type=MESH
            )
        total += size - 1
    pl.semaphore_wait(barrier, total)


def start_exchange(axis, source, target, sems):
    size = lax.axis_size(axis)
    me = lax.axis_index(axis)
    copies = []
    for step in range(1, size):
        peer = lax.rem(me + step, size)
        copy = pltpu.make_async_remote_copy(
            src_ref=source(peer),
            dst_ref=target,
            send_sem=sems.at[0, step - 1],
            recv_sem=sems.at[1, step - 1],
            device_id={axis: peer},
            device_id_type=MESH,
        )
        copy.start()
        copies.append(copy)
    return copies


def wait_all(copies):
    for copy in copies:
        copy.wait()


def exchange(axis, source, target, sems):
    wait_all(start_exchange(axis, source, target, sems))


def sem_pair(axis):
    return pltpu.SemaphoreType.DMA((2, lax.axis_size(axis) - 1))


def call(kernel, outs, scratch, number, *args):
    return pl.pallas_call(
        kernel,
        out_shape=outs,
        in_specs=[VMEM] * len(args),
        out_specs=jax.tree.map(lambda _: VMEM, outs),
        scratch_shapes=scratch,
        compiler_params=pltpu.CompilerParams(
            collective_id=number, has_side_effects=True, vmem_limit_bytes=48 * 2**20
        ),
    )(*args)


def modulation_kernel(
    cond_ref, w_ref, x_ref, shard_ref, mod_ref, act_ref, x_all, w_all,
    cond_buf, part, recv, own, s0, s1, s2, s3, s4, s5
):
    count = lax.axis_size("dp")
    me, mine = lax.axis_index("dp"), lax.axis_index("tensor")
    greet(("dp", "tensor"))
    copies = start_exchange("dp", lambda peer: cond_ref.at[peer], cond_buf.at[me], s0)
    x_own = token_block(x_all, mine, x_ref.shape[1])
    x_copies = start_exchange("tensor", lambda peer: x_ref, x_own, s3)
    cond_buf[me] = cond_ref[me]
    x_own[...] = x_ref[...]
    w_all[me] = shard_ref[...]
    wait_all(copies)

    @pl.loop(0, count)
    def _(at):
        act = silu_value(cond_buf[at]).astype(bf16)
        act_ref[at] = act.astype(f32)
        part[at] = jnp.dot(act, w_ref[...], preferred_element_type=f32)

    copies = start_exchange("dp", lambda peer: part.at[peer], recv.at[me], s1)
    recv[me] = part[me]
    pairs = count // 2
    chip, side = me // 2, lax.rem(me, 2)
    sibling = 2 * chip + 1 - side

    def send(source, at, to, sems, number):
        copy = pltpu.make_async_remote_copy(
            src_ref=source,
            dst_ref=w_all.at[at],
            send_sem=sems.at[0, number],
            recv_sem=sems.at[1, number],
            device_id={"dp": to},
            device_id_type=MESH,
        )
        copy.start()
        return copy

    far = [
        send(shard_ref, me, 2 * lax.rem(chip + step, pairs) + side, s4, step)
        for step in range(1, pairs)
    ]
    near = [send(shard_ref, me, sibling, s5, 0)]
    wait_all(copies)
    own[...] = jnp.sum(recv[...], axis=0)
    copies = start_exchange("tensor", lambda peer: own, mod_ref.at[mine], s2)
    mod_ref[mine] = own[...]
    for step in range(1, pairs):
        far[step - 1].wait()
        came = 2 * lax.rem(chip + pairs - step, pairs) + side
        near.append(send(w_all.at[came], came, sibling, s5, step))
    wait_all(near)
    wait_all(copies)
    wait_all(x_copies)


def modulation_of(condition, w_ada, block, shard):
    count, group = lax.axis_size("dp"), lax.axis_size("tensor")
    rows, width = condition.shape
    shard_rows, columns = w_ada.shape
    blocks = condition.astype(f32).reshape(rows, count, shard_rows).transpose(1, 0, 2)
    mod, act, x_all, w_all = call(
        modulation_kernel,
        (
            jax.ShapeDtypeStruct((group, rows, columns), f32),
            jax.ShapeDtypeStruct((count, rows, shard_rows), f32),
            jax.ShapeDtypeStruct((rows, group * block.shape[1], width), bf16),
            jax.ShapeDtypeStruct((count,) + shard.shape, bf16),
        ),
        [
            pltpu.VMEM((count, rows, shard_rows), f32),
            pltpu.VMEM((count, rows, columns), f32),
            pltpu.VMEM((count, rows, columns), f32),
            pltpu.VMEM((rows, columns), f32),
            sem_pair("dp"),
            sem_pair("dp"),
            sem_pair("tensor"),
            sem_pair("tensor"),
            pltpu.SemaphoreType.DMA((2, count // 2)),
            pltpu.SemaphoreType.DMA((2, count // 2)),
        ],
        1,
        blocks,
        w_ada,
        block,
        shard,
    )
    mod = mod.transpose(1, 0, 2).reshape(rows, group * columns)
    act = act.reshape(count * rows, shard_rows).astype(bf16)
    return mod, act, x_all, w_all.reshape(count * shard.shape[0], shard.shape[1])


def token_block(ref, at, size):
    return ref.at[:, pl.ds(pl.multiple_of(at * size, size), size)]


def reduce_kernel(part_ref, out_ref, recv, s0, s1):
    group = lax.axis_size("tensor")
    mine = lax.axis_index("tensor")
    size = part_ref.shape[1] // group
    greet(("tensor",))
    exchange("tensor", lambda peer: token_block(part_ref, peer, size), recv.at[mine], s0)
    total = token_block(part_ref, mine, size)[...].astype(f32)
    for step in range(1, group):
        total += recv[lax.rem(mine + step, group)].astype(f32)
    own = token_block(out_ref, mine, size)
    own[...] = total.astype(bf16)
    exchange("tensor", lambda peer: own, own, s1)


def reduce_tensor(part, number):
    group = lax.axis_size("tensor")
    rows, seq, width = part.shape
    return call(
        reduce_kernel,
        jax.ShapeDtypeStruct(part.shape, bf16),
        [
            pltpu.VMEM((group, rows, seq // group, width), bf16),
            sem_pair("tensor"),
            sem_pair("tensor"),
        ],
        number,
        part.astype(bf16),
    ).astype(f32)


def final_kernel(
    attn_ref, ffn_ref, grad_ref, part_ref, w_ref, attn_out, ffn_out, grad_out, all_ref, act_ref,
    attn_recv, ffn_recv, pair_recv, stage, grad_recv, recv_mod, own, part, terms, gathered,
    s0, s1, s2, s3, m0, m1, m2, m3
):
    group = lax.axis_size("tensor")
    count = lax.axis_size("dp")
    pairs = count // 2
    me, mine = lax.axis_index("dp"), lax.axis_index("tensor")
    chip, side = me // 2, lax.rem(me, 2)
    size = attn_ref.shape[1] // group
    greet(("dp", "tensor"))
    copies = start_exchange("tensor", lambda peer: part_ref.at[peer], recv_mod.at[mine], m0)
    recv_mod[mine] = part_ref[mine]
    pair_copy = pltpu.make_async_remote_copy(
        src_ref=grad_ref.at[:, 1 - side],
        dst_ref=pair_recv,
        send_sem=s0.at[0],
        recv_sem=s0.at[1],
        device_id={"dp": 2 * chip + 1 - side},
        device_id_type=MESH,
    )
    pair_copy.start()
    attn_copies = start_exchange(
        "tensor", lambda peer: token_block(attn_ref, peer, size), attn_recv.at[mine], s1
    )
    ffn_copies = start_exchange(
        "tensor", lambda peer: token_block(ffn_ref, peer, size), ffn_recv.at[mine], s2
    )
    wait_all(copies)
    own[...] = jnp.sum(recv_mod[...], axis=0).astype(bf16).astype(f32)
    copies = start_exchange("dp", lambda peer: own, all_ref.at[me], m1)
    all_ref[me] = own[...]
    wait_all(copies)

    @pl.loop(0, count)
    def _(at):
        part[at] = lax.dot_general(
            all_ref[at].astype(bf16),
            w_ref[...],
            (((1,), (1,)), ((), ())),
            preferred_element_type=f32,
        )

    copies = start_exchange("dp", lambda peer: part.at[peer], terms.at[me], m2)
    terms[me] = part[me]
    pair_copy.wait()
    grad_copies = []
    for step in range(pairs):
        to = lax.rem(chip + step, pairs) if step else chip
        total = grad_ref[to, side].astype(f32) + pair_recv[to].astype(f32)
        if step == 0:
            grad_out[...] = total
            continue
        stage[to] = total.astype(bf16)
        copy = pltpu.make_async_remote_copy(
            src_ref=stage.at[to],
            dst_ref=grad_recv.at[chip],
            send_sem=s3.at[0, step - 1],
            recv_sem=s3.at[1, step - 1],
            device_id={"dp": 2 * to + side},
            device_id_type=MESH,
        )
        copy.start()
        grad_copies.append(copy)
    wait_all(copies)
    last_copies = start_exchange("tensor", lambda peer: terms, gathered.at[mine], m3)
    gathered[mine] = terms[...]
    wait_all(grad_copies)
    for step in range(1, pairs):
        grad_out[...] += grad_recv[lax.rem(chip + step, pairs)].astype(f32)
    for copies, source, recv, out in (
        (attn_copies, attn_ref, attn_recv, attn_out),
        (ffn_copies, ffn_ref, ffn_recv, ffn_out),
    ):
        wait_all(copies)
        total = token_block(source, mine, size)[...].astype(f32)
        for step in range(1, group):
            total += recv[lax.rem(mine + step, group)].astype(f32)
        out[...] = total
    wait_all(last_copies)
    act_ref[...] = jnp.sum(gathered[...], axis=0)


def final_sums(attn_part, ffn_part, grads, parts, w_ada):
    group, count = lax.axis_size("tensor"), lax.axis_size("dp")
    rows, seq, width = attn_part.shape
    depth, columns = grads.shape
    shard_rows = depth // count
    tokens = (rows, seq // group, width)
    mod_columns = w_ada.shape[1]
    attn_own, ffn_own, grads, everyone, act = call(
        final_kernel,
        (
            jax.ShapeDtypeStruct(tokens, f32),
            jax.ShapeDtypeStruct(tokens, f32),
            jax.ShapeDtypeStruct((shard_rows, columns), f32),
            jax.ShapeDtypeStruct((count, rows, mod_columns), f32),
            jax.ShapeDtypeStruct((count, rows, shard_rows), f32),
        ),
        [
            pltpu.VMEM((group,) + tokens, bf16),
            pltpu.VMEM((group,) + tokens, bf16),
            pltpu.VMEM((count // 2, shard_rows, columns), bf16),
            pltpu.VMEM((count // 2, shard_rows, columns), bf16),
            pltpu.VMEM((count // 2, shard_rows, columns), bf16),
            pltpu.VMEM((group, rows, mod_columns), f32),
            pltpu.VMEM((rows, mod_columns), f32),
            pltpu.VMEM((count, rows, shard_rows), f32),
            pltpu.VMEM((count, rows, shard_rows), f32),
            pltpu.VMEM((group, count, rows, shard_rows), f32),
            pltpu.SemaphoreType.DMA((2,)),
            sem_pair("tensor"),
            sem_pair("tensor"),
            pltpu.SemaphoreType.DMA((2, count // 2 - 1)),
            sem_pair("tensor"),
            sem_pair("dp"),
            sem_pair("dp"),
            sem_pair("tensor"),
        ],
        5,
        attn_part.astype(bf16),
        ffn_part.astype(bf16),
        grads.astype(bf16).reshape(count // 2, 2, shard_rows, columns),
        parts.reshape(rows, group, mod_columns).transpose(1, 0, 2),
        w_ada,
    )
    everyone = everyone.reshape(count * rows, mod_columns).astype(bf16)
    d_act = act.transpose(1, 0, 2).reshape(rows, count * shard_rows)
    return attn_own, ffn_own, grads, everyone, d_act


def shards(latent_in, condition, w_ada, w_qkv, w_proj, w_up, w_down, out_grad):
    rows, own_tokens, width = latent_in.shape
    scale = HEAD_DIM ** (-0.5)
    tensor_at = lax.axis_index("tensor")
    local = w_proj.shape[0]
    heads = local // HEAD_DIM
    units = w_down.shape[0]

    attn_shard = jnp.concatenate(
        [w_qkv[0], w_qkv[1], w_qkv[2], w_proj.T], axis=1
    )
    ffn_shard = jnp.concatenate([w_up, w_down.T], axis=1)
    modulation, cond_mine, tokens, attn_weights = modulation_of(
        condition, w_ada, latent_in, attn_shard
    )
    modulation = modulation.reshape(rows, 6, 1, width)
    shift_a, scale_a, gate_a, shift_f, scale_f, gate_f = (modulation[:, i] for i in range(6))

    w_in = attn_weights[:, : 3 * local]
    proj_t = attn_weights[:, 3 * local :]
    cotangent = gather_tensor(out_grad, 1).astype(f32)
    ffn_weights = gather_weights(ffn_shard)
    up = ffn_weights[:, :units]
    down_t = ffn_weights[:, units:]

    tokens = tokens.astype(f32)
    seq = tokens.shape[1]

    normed_a, inverse_a = norm_parts(tokens)
    attn_in = (normed_a * (1.0 + scale_a) + shift_a).astype(bf16)
    projected = dot("lsd,de->lse", attn_in, w_in).astype(bf16)
    projected = projected.reshape(rows, seq, 3, heads, HEAD_DIM)
    queries, keys, values = projected[:, :, 0], projected[:, :, 1], projected[:, :, 2]
    scores = dot("lqhe,lkhe->lhqk", queries, keys) * scale
    shifted = jnp.exp(scores - jnp.max(scores, axis=-1, keepdims=True))
    probs = shifted / jnp.sum(shifted, axis=-1, keepdims=True)
    probs_low = probs.astype(bf16)
    mixed = dot("lhqk,lkhe->lqhe", probs_low, values).reshape(rows, seq, local).astype(bf16)
    attn_out = reduce_tensor(dot("lsd,ed->lse", mixed, proj_t), 3)
    resid = tokens + gate_a * attn_out
    normed_f, inverse_f = norm_parts(resid)
    ffn_in = (normed_f * (1.0 + scale_f) + shift_f).astype(bf16)
    hidden_pre = dot("lsd,dn->lsn", ffn_in, up)
    hidden, gelu_pull = jax.vjp(gelu_tanh, hidden_pre)
    hidden = hidden.astype(bf16)
    d_ffn_out = (gate_f * cotangent).astype(bf16)
    d_hidden_pre = gelu_pull(dot("lse,en->lsn", d_ffn_out, down_t))[0].astype(bf16)
    d_ffn_in = reduce_tensor(dot("lsn,dn->lsd", d_hidden_pre, up), 4)

    ffn_part = dot("lsn,en->lse", hidden, down_t)
    d_gate_f = jnp.sum(cotangent * ffn_part, axis=1)
    d_shift_f = jnp.sum(d_ffn_in, axis=1)
    d_scale_f = jnp.sum(d_ffn_in * normed_f, axis=1)
    d_resid = cotangent + norm_back(normed_f, inverse_f, d_ffn_in * (1.0 + scale_f))
    d_gate_a = jnp.sum(d_resid * attn_out, axis=1)
    d_attn_out = (gate_a * d_resid).astype(bf16)
    d_mixed = dot("lse,ed->lsd", d_attn_out, proj_t).astype(bf16)
    d_mixed = d_mixed.reshape(rows, seq, heads, HEAD_DIM)
    d_probs = dot("lqhe,lkhe->lhqk", d_mixed, values)
    d_scores = probs * (d_probs - jnp.sum(d_probs * probs, axis=-1, keepdims=True))
    d_scores = d_scores.astype(bf16)
    d_values = dot("lhqk,lqhe->lkhe", probs_low, d_mixed)
    d_queries = dot("lhqk,lkhe->lqhe", d_scores, keys) * scale
    d_keys = dot("lhqk,lqhe->lkhe", d_scores, queries) * scale
    d_projected = jnp.stack([d_queries, d_keys, d_values], axis=2)
    d_projected = d_projected.reshape(rows, seq, 3 * local).astype(bf16)
    d_attn_part = dot("lse,de->lsd", d_projected, w_in)

    grads = jnp.concatenate(
        [
            dot("lsd,lse->de", attn_in, d_projected).astype(bf16),
            dot("lse,lsd->ed", d_attn_out, mixed).astype(bf16),
            dot("lsd,lsn->dn", ffn_in, d_hidden_pre).astype(bf16),
            dot("lse,lsn->en", d_ffn_out, hidden).astype(bf16),
        ],
        axis=1,
    )
    d_shift_a = jnp.sum(d_attn_part, axis=1)
    d_scale_a = jnp.sum(d_attn_part * normed_a, axis=1)
    ones = jnp.where(tensor_at == 0, 1.0, 0.0)
    d_modulation = jnp.concatenate(
        [d_shift_a, d_scale_a, d_gate_a * ones, d_shift_f * ones, d_scale_f * ones, d_gate_f],
        axis=1,
    )
    d_attn_own, ffn_own, grads, d_mod_all, d_act = final_sums(
        d_attn_part, ffn_part, grads, d_modulation, w_ada
    )
    grad_attn, grad_ffn = grads[:, : 4 * local], grads[:, 4 * local :]
    first = tensor_at * own_tokens
    own = lambda value: lax.dynamic_slice_in_dim(value, first, own_tokens, 1)
    latent_out = (own(resid) + gate_f * ffn_own).astype(bf16)
    grad_latent = own(d_resid) + norm_back(
        own(normed_a), own(inverse_a), d_attn_own * (1.0 + scale_a)
    )

    grad_ada = dot("ld,le->de", cond_mine, d_mod_all)
    grad_condition = jax.vjp(silu_value, condition.astype(f32))[1](d_act)[0]

    grad_qkv = jnp.stack([grad_attn[:, j * local : (j + 1) * local] for j in range(3)], axis=0)
    grad_proj = grad_attn[:, 3 * local :].T
    grad_up = grad_ffn[:, :units]
    grad_down = grad_ffn[:, units:].T
    return (
        latent_out,
        grad_latent,
        grad_condition,
        grad_ada,
        grad_qkv,
        grad_proj,
        grad_up,
        grad_down,
    )


def solution(mesh):
    return jax.shard_map(
        shards,
        mesh=mesh,
        in_specs=(
            P("dp", "tensor", None),
            P("dp", None),
            P("dp", "tensor"),
            P(None, "dp", "tensor"),
            P("tensor", "dp"),
            P("dp", "tensor"),
            P("tensor", "dp"),
            P("dp", "tensor", None),
        ),
        out_specs=(
            P("dp", "tensor", None),
            P("dp", "tensor", None),
            P("dp", None),
            P("dp", "tensor"),
            P(None, "dp", "tensor"),
            P("tensor", "dp"),
            P("dp", "tensor"),
            P("tensor", "dp"),
        ),
        check_vma=False,
    )
```

```python
import math

import jax
import jax.numpy as jnp
from jax import lax
from jax.experimental import pallas as pl
from jax.experimental.pallas import tpu as pltpu
from jax.sharding import PartitionSpec as P

MESH = pl.DeviceIdType.MESH
VMEM = pl.BlockSpec(memory_space=pltpu.VMEM)

HEAD_DIM = 64
EPS = 1e-06
f32 = jnp.float32
bf16 = jnp.bfloat16


def silu_value(values):
    return values / (1.0 + jnp.exp(-values))


def gelu_tanh(values):
    return (
        0.5
        * values
        * (
            1.0
            + jnp.tanh(math.sqrt(2.0 / math.pi) * (values + 0.044715 * values * values * values))
        )
    )


def norm_parts(values):
    centered = values - jnp.mean(values, axis=-1, keepdims=True)
    variance = jnp.mean(centered * centered, axis=-1, keepdims=True)
    inverse = lax.rsqrt(variance + EPS)
    return centered * inverse, inverse


def norm_back(normed, inverse, grad):
    return inverse * (
        grad
        - jnp.mean(grad, axis=-1, keepdims=True)
        - normed * jnp.mean(grad * normed, axis=-1, keepdims=True)
    )


def dot(form, left, right):
    return jnp.einsum(form, left, right, preferred_element_type=f32)


def gather_tensor(block, axis):
    return lax.all_gather(block, "tensor", axis=axis, tiled=True)


def greet(axes):
    barrier = pltpu.get_barrier_semaphore()
    total = 0
    for axis in axes:
        size = lax.axis_size(axis)
        me = lax.axis_index(axis)
        for step in range(1, size):
            pl.semaphore_signal(
                barrier, inc=1, device_id={axis: lax.rem(me + step, size)}, device_id_type=MESH
            )
        total += size - 1
    pl.semaphore_wait(barrier, total)


def start_exchange(axis, source, target, sems):
    size = lax.axis_size(axis)
    me = lax.axis_index(axis)
    copies = []
    for step in range(1, size):
        peer = lax.rem(me + step, size)
        copy = pltpu.make_async_remote_copy(
            src_ref=source(peer),
            dst_ref=target,
            send_sem=sems.at[0, step - 1],
            recv_sem=sems.at[1, step - 1],
            device_id={axis: peer},
            device_id_type=MESH,
        )
        copy.start()
        copies.append(copy)
    return copies


def wait_all(copies):
    for copy in copies:
        copy.wait()


def exchange(axis, source, target, sems):
    wait_all(start_exchange(axis, source, target, sems))


def sem_pair(axis):
    return pltpu.SemaphoreType.DMA((2, lax.axis_size(axis) - 1))


def call(kernel, outs, scratch, number, *args):
    return pl.pallas_call(
        kernel,
        out_shape=outs,
        in_specs=[VMEM] * len(args),
        out_specs=jax.tree.map(lambda _: VMEM, outs),
        scratch_shapes=scratch,
        compiler_params=pltpu.CompilerParams(
            collective_id=number, has_side_effects=True, vmem_limit_bytes=48 * 2**20
        ),
    )(*args)


def modulation_kernel(
    cond_ref, w_ref, x_ref, shard_ref, mod_ref, act_ref, x_all, w_all,
    cond_buf, part, recv, own, s0, s1, s2, s3, s4, s5
):
    count = lax.axis_size("dp")
    me, mine = lax.axis_index("dp"), lax.axis_index("tensor")
    greet(("dp", "tensor"))
    copies = start_exchange("dp", lambda peer: cond_ref.at[peer], cond_buf.at[me], s0)
    x_own = token_block(x_all, mine, x_ref.shape[1])
    x_copies = start_exchange("tensor", lambda peer: x_ref, x_own, s3)
    cond_buf[me] = cond_ref[me]
    x_own[...] = x_ref[...]
    w_all[me] = shard_ref[...]
    wait_all(copies)

    @pl.loop(0, count)
    def _(at):
        act = silu_value(cond_buf[at]).astype(bf16)
        act_ref[at] = act.astype(f32)
        part[at] = jnp.dot(act, w_ref[...], preferred_element_type=f32)

    copies = start_exchange("dp", lambda peer: part.at[peer], recv.at[me], s1)
    recv[me] = part[me]
    pairs = count // 2
    chip, side = me // 2, lax.rem(me, 2)
    sibling = 2 * chip + 1 - side

    def send(source, at, to, sems, number):
        copy = pltpu.make_async_remote_copy(
            src_ref=source,
            dst_ref=w_all.at[at],
            send_sem=sems.at[0, number],
            recv_sem=sems.at[1, number],
            device_id={"dp": to},
            device_id_type=MESH,
        )
        copy.start()
        return copy

    far = [
        send(shard_ref, me, 2 * lax.rem(chip + step, pairs) + side, s4, step)
        for step in range(1, pairs)
    ]
    near = [send(shard_ref, me, sibling, s5, 0)]
    wait_all(copies)
    own[...] = jnp.sum(recv[...], axis=0)
    copies = start_exchange("tensor", lambda peer: own, mod_ref.at[mine], s2)
    mod_ref[mine] = own[...]
    for step in range(1, pairs):
        far[step - 1].wait()
        came = 2 * lax.rem(chip + pairs - step, pairs) + side
        near.append(send(w_all.at[came], came, sibling, s5, step))
    wait_all(near)
    wait_all(copies)
    wait_all(x_copies)


def modulation_of(condition, w_ada, block, shard):
    count, group = lax.axis_size("dp"), lax.axis_size("tensor")
    rows, width = condition.shape
    shard_rows, columns = w_ada.shape
    blocks = condition.astype(f32).reshape(rows, count, shard_rows).transpose(1, 0, 2)
    mod, act, x_all, w_all = call(
        modulation_kernel,
        (
            jax.ShapeDtypeStruct((group, rows, columns), f32),
            jax.ShapeDtypeStruct((count, rows, shard_rows), f32),
            jax.ShapeDtypeStruct((rows, group * block.shape[1], width), bf16),
            jax.ShapeDtypeStruct((count,) + shard.shape, bf16),
        ),
        [
            pltpu.VMEM((count, rows, shard_rows), f32),
            pltpu.VMEM((count, rows, columns), f32),
            pltpu.VMEM((count, rows, columns), f32),
            pltpu.VMEM((rows, columns), f32),
            sem_pair("dp"),
            sem_pair("dp"),
            sem_pair("tensor"),
            sem_pair("tensor"),
            pltpu.SemaphoreType.DMA((2, count // 2)),
            pltpu.SemaphoreType.DMA((2, count // 2)),
        ],
        1,
        blocks,
        w_ada,
        block,
        shard,
    )
    mod = mod.transpose(1, 0, 2).reshape(rows, group * columns)
    act = act.reshape(count * rows, shard_rows).astype(bf16)
    return mod, act, x_all, w_all.reshape(count * shard.shape[0], shard.shape[1])


def token_block(ref, at, size):
    return ref.at[:, pl.ds(pl.multiple_of(at * size, size), size)]


def finish_reduce(part_ref, out_ref, recv, first, sems):
    group = lax.axis_size("tensor")
    mine = lax.axis_index("tensor")
    size = part_ref.shape[1] // group
    wait_all(first)
    total = token_block(part_ref, mine, size)[...].astype(f32)
    for step in range(1, group):
        total += recv[lax.rem(mine + step, group)].astype(f32)
    own = token_block(out_ref, mine, size)
    own[...] = total.astype(bf16)
    return start_exchange("tensor", lambda peer: own, own, sems)


def start_reduce(part_ref, recv, sems):
    group = lax.axis_size("tensor")
    size = part_ref.shape[1] // group
    return start_exchange(
        "tensor",
        lambda peer: token_block(part_ref, peer, size),
        recv.at[lax.axis_index("tensor")],
        sems,
    )


def reduce_kernel(part_ref, out_ref, recv, s0, s1):
    greet(("tensor",))
    first = start_reduce(part_ref, recv, s0)
    wait_all(finish_reduce(part_ref, out_ref, recv, first, s1))


def reduce_gather_kernel(part_ref, shard_ref, out_ref, w_all, recv, s0, s1, s2, s3):
    count = lax.axis_size("dp")
    me = lax.axis_index("dp")
    pairs = count // 2
    chip, side = me // 2, lax.rem(me, 2)
    sibling = 2 * chip + 1 - side
    greet(("dp", "tensor"))

    def send(source, at, to, sems, number):
        copy = pltpu.make_async_remote_copy(
            src_ref=source,
            dst_ref=w_all.at[at],
            send_sem=sems.at[0, number],
            recv_sem=sems.at[1, number],
            device_id={"dp": to},
            device_id_type=MESH,
        )
        copy.start()
        return copy

    first = start_reduce(part_ref, recv, s0)
    far = [
        send(shard_ref, me, 2 * lax.rem(chip + step, pairs) + side, s2, step)
        for step in range(1, pairs)
    ]
    near = [send(shard_ref, me, sibling, s3, 0)]
    w_all[me] = shard_ref[...]
    last = finish_reduce(part_ref, out_ref, recv, first, s1)
    for step in range(1, pairs):
        far[step - 1].wait()
        came = 2 * lax.rem(chip + pairs - step, pairs) + side
        near.append(send(w_all.at[came], came, sibling, s3, step))
    wait_all(near)
    wait_all(last)


def reduce_and_gather(part, shard, number):
    group, count = lax.axis_size("tensor"), lax.axis_size("dp")
    rows, seq, width = part.shape
    total, weights = call(
        reduce_gather_kernel,
        (
            jax.ShapeDtypeStruct(part.shape, bf16),
            jax.ShapeDtypeStruct((count,) + shard.shape, bf16),
        ),
        [
            pltpu.VMEM((group, rows, seq // group, width), bf16),
            sem_pair("tensor"),
            sem_pair("tensor"),
            pltpu.SemaphoreType.DMA((2, count // 2)),
            pltpu.SemaphoreType.DMA((2, count // 2)),
        ],
        number,
        part.astype(bf16),
        shard,
    )
    return total.astype(f32), weights.reshape(count * shard.shape[0], shard.shape[1])


def reduce_tensor(part, number):
    group = lax.axis_size("tensor")
    rows, seq, width = part.shape
    return call(
        reduce_kernel,
        jax.ShapeDtypeStruct(part.shape, bf16),
        [
            pltpu.VMEM((group, rows, seq // group, width), bf16),
            sem_pair("tensor"),
            sem_pair("tensor"),
        ],
        number,
        part.astype(bf16),
    ).astype(f32)


def final_kernel(
    attn_ref, ffn_ref, grad_ref, part_ref, w_ref, attn_out, ffn_out, grad_out, all_ref, act_ref,
    attn_recv, ffn_recv, pair_recv, stage, grad_recv, recv_mod, own, part, terms, gathered,
    s0, s1, s2, s3, m0, m1, m2, m3
):
    group = lax.axis_size("tensor")
    count = lax.axis_size("dp")
    pairs = count // 2
    me, mine = lax.axis_index("dp"), lax.axis_index("tensor")
    chip, side = me // 2, lax.rem(me, 2)
    size = attn_ref.shape[1] // group
    greet(("dp", "tensor"))
    copies = start_exchange("tensor", lambda peer: part_ref.at[peer], recv_mod.at[mine], m0)
    recv_mod[mine] = part_ref[mine]
    pair_copy = pltpu.make_async_remote_copy(
        src_ref=grad_ref.at[:, 1 - side],
        dst_ref=pair_recv,
        send_sem=s0.at[0],
        recv_sem=s0.at[1],
        device_id={"dp": 2 * chip + 1 - side},
        device_id_type=MESH,
    )
    pair_copy.start()
    attn_copies = start_exchange(
        "tensor", lambda peer: token_block(attn_ref, peer, size), attn_recv.at[mine], s1
    )
    ffn_copies = start_exchange(
        "tensor", lambda peer: token_block(ffn_ref, peer, size), ffn_recv.at[mine], s2
    )
    wait_all(copies)
    own[...] = jnp.sum(recv_mod[...], axis=0).astype(bf16).astype(f32)
    copies = start_exchange("dp", lambda peer: own, all_ref.at[me], m1)
    all_ref[me] = own[...]
    wait_all(copies)

    @pl.loop(0, count)
    def _(at):
        part[at] = lax.dot_general(
            all_ref[at].astype(bf16),
            w_ref[...],
            (((1,), (1,)), ((), ())),
            preferred_element_type=f32,
        )

    copies = start_exchange("dp", lambda peer: part.at[peer], terms.at[me], m2)
    terms[me] = part[me]
    pair_copy.wait()
    grad_copies = []
    for step in range(pairs):
        to = lax.rem(chip + step, pairs) if step else chip
        total = grad_ref[to, side].astype(f32) + pair_recv[to].astype(f32)
        if step == 0:
            grad_out[...] = total
            continue
        stage[to] = total.astype(bf16)
        copy = pltpu.make_async_remote_copy(
            src_ref=stage.at[to],
            dst_ref=grad_recv.at[chip],
            send_sem=s3.at[0, step - 1],
            recv_sem=s3.at[1, step - 1],
            device_id={"dp": 2 * to + side},
            device_id_type=MESH,
        )
        copy.start()
        grad_copies.append(copy)
    wait_all(copies)
    last_copies = start_exchange("tensor", lambda peer: terms, gathered.at[mine], m3)
    gathered[mine] = terms[...]
    wait_all(grad_copies)
    for step in range(1, pairs):
        grad_out[...] += grad_recv[lax.rem(chip + step, pairs)].astype(f32)
    for copies, source, recv, out in (
        (attn_copies, attn_ref, attn_recv, attn_out),
        (ffn_copies, ffn_ref, ffn_recv, ffn_out),
    ):
        wait_all(copies)
        total = token_block(source, mine, size)[...].astype(f32)
        for step in range(1, group):
            total += recv[lax.rem(mine + step, group)].astype(f32)
        out[...] = total
    wait_all(last_copies)
    act_ref[...] = jnp.sum(gathered[...], axis=0)


def final_sums(attn_part, ffn_part, grads, parts, w_ada):
    group, count = lax.axis_size("tensor"), lax.axis_size("dp")
    rows, seq, width = attn_part.shape
    depth, columns = grads.shape
    shard_rows = depth // count
    tokens = (rows, seq // group, width)
    mod_columns = w_ada.shape[1]
    attn_own, ffn_own, grads, everyone, act = call(
        final_kernel,
        (
            jax.ShapeDtypeStruct(tokens, f32),
            jax.ShapeDtypeStruct(tokens, f32),
            jax.ShapeDtypeStruct((shard_rows, columns), f32),
            jax.ShapeDtypeStruct((count, rows, mod_columns), f32),
            jax.ShapeDtypeStruct((count, rows, shard_rows), f32),
        ),
        [
            pltpu.VMEM((group,) + tokens, bf16),
            pltpu.VMEM((group,) + tokens, bf16),
            pltpu.VMEM((count // 2, shard_rows, columns), bf16),
            pltpu.VMEM((count // 2, shard_rows, columns), bf16),
            pltpu.VMEM((count // 2, shard_rows, columns), bf16),
            pltpu.VMEM((group, rows, mod_columns), f32),
            pltpu.VMEM((rows, mod_columns), f32),
            pltpu.VMEM((count, rows, shard_rows), f32),
            pltpu.VMEM((count, rows, shard_rows), f32),
            pltpu.VMEM((group, count, rows, shard_rows), f32),
            pltpu.SemaphoreType.DMA((2,)),
            sem_pair("tensor"),
            sem_pair("tensor"),
            pltpu.SemaphoreType.DMA((2, count // 2 - 1)),
            sem_pair("tensor"),
            sem_pair("dp"),
            sem_pair("dp"),
            sem_pair("tensor"),
        ],
        5,
        attn_part.astype(bf16),
        ffn_part.astype(bf16),
        grads.astype(bf16).reshape(count // 2, 2, shard_rows, columns),
        parts.reshape(rows, group, mod_columns).transpose(1, 0, 2),
        w_ada,
    )
    everyone = everyone.reshape(count * rows, mod_columns).astype(bf16)
    d_act = act.transpose(1, 0, 2).reshape(rows, count * shard_rows)
    return attn_own, ffn_own, grads, everyone, d_act


def shards(latent_in, condition, w_ada, w_qkv, w_proj, w_up, w_down, out_grad):
    rows, own_tokens, width = latent_in.shape
    scale = HEAD_DIM ** (-0.5)
    tensor_at = lax.axis_index("tensor")
    local = w_proj.shape[0]
    heads = local // HEAD_DIM
    units = w_down.shape[0]

    attn_shard = jnp.concatenate(
        [w_qkv[0], w_qkv[1], w_qkv[2], w_proj.T], axis=1
    )
    ffn_shard = jnp.concatenate([w_up, w_down.T], axis=1)
    modulation, cond_mine, tokens, attn_weights = modulation_of(
        condition, w_ada, latent_in, attn_shard
    )
    modulation = modulation.reshape(rows, 6, 1, width)
    shift_a, scale_a, gate_a, shift_f, scale_f, gate_f = (modulation[:, i] for i in range(6))

    w_in = attn_weights[:, : 3 * local]
    proj_t = attn_weights[:, 3 * local :]
    cotangent = gather_tensor(out_grad, 1).astype(f32)
    tokens = tokens.astype(f32)
    seq = tokens.shape[1]

    normed_a, inverse_a = norm_parts(tokens)
    attn_in = (normed_a * (1.0 + scale_a) + shift_a).astype(bf16)
    projected = dot("lsd,de->lse", attn_in, w_in).astype(bf16)
    projected = projected.reshape(rows, seq, 3, heads, HEAD_DIM)
    queries, keys, values = projected[:, :, 0], projected[:, :, 1], projected[:, :, 2]
    scores = dot("lqhe,lkhe->lhqk", queries, keys) * scale
    shifted = jnp.exp(scores - jnp.max(scores, axis=-1, keepdims=True))
    probs = shifted / jnp.sum(shifted, axis=-1, keepdims=True)
    probs_low = probs.astype(bf16)
    mixed = dot("lhqk,lkhe->lqhe", probs_low, values).reshape(rows, seq, local).astype(bf16)
    attn_out, ffn_weights = reduce_and_gather(dot("lsd,ed->lse", mixed, proj_t), ffn_shard, 3)
    up = ffn_weights[:, :units]
    down_t = ffn_weights[:, units:]
    resid = tokens + gate_a * attn_out
    normed_f, inverse_f = norm_parts(resid)
    ffn_in = (normed_f * (1.0 + scale_f) + shift_f).astype(bf16)
    hidden_pre = dot("lsd,dn->lsn", ffn_in, up)
    hidden, gelu_pull = jax.vjp(gelu_tanh, hidden_pre)
    hidden = hidden.astype(bf16)
    d_ffn_out = (gate_f * cotangent).astype(bf16)
    d_hidden_pre = gelu_pull(dot("lse,en->lsn", d_ffn_out, down_t))[0].astype(bf16)
    d_ffn_in = reduce_tensor(dot("lsn,dn->lsd", d_hidden_pre, up), 4)

    ffn_part = dot("lsn,en->lse", hidden, down_t)
    d_gate_f = jnp.sum(cotangent * ffn_part, axis=1)
    d_shift_f = jnp.sum(d_ffn_in, axis=1)
    d_scale_f = jnp.sum(d_ffn_in * normed_f, axis=1)
    d_resid = cotangent + norm_back(normed_f, inverse_f, d_ffn_in * (1.0 + scale_f))
    d_gate_a = jnp.sum(d_resid * attn_out, axis=1)
    d_attn_out = (gate_a * d_resid).astype(bf16)
    d_mixed = dot("lse,ed->lsd", d_attn_out, proj_t).astype(bf16)
    d_mixed = d_mixed.reshape(rows, seq, heads, HEAD_DIM)
    d_probs = dot("lqhe,lkhe->lhqk", d_mixed, values)
    d_scores = probs * (d_probs - jnp.sum(d_probs * probs, axis=-1, keepdims=True))
    d_scores = d_scores.astype(bf16)
    d_values = dot("lhqk,lqhe->lkhe", probs_low, d_mixed)
    d_queries = dot("lhqk,lkhe->lqhe", d_scores, keys) * scale
    d_keys = dot("lhqk,lqhe->lkhe", d_scores, queries) * scale
    d_projected = jnp.stack([d_queries, d_keys, d_values], axis=2)
    d_projected = d_projected.reshape(rows, seq, 3 * local).astype(bf16)
    d_attn_part = dot("lse,de->lsd", d_projected, w_in)

    grads = jnp.concatenate(
        [
            dot("lsd,lse->de", attn_in, d_projected).astype(bf16),
            dot("lse,lsd->ed", d_attn_out, mixed).astype(bf16),
            dot("lsd,lsn->dn", ffn_in, d_hidden_pre).astype(bf16),
            dot("lse,lsn->en", d_ffn_out, hidden).astype(bf16),
        ],
        axis=1,
    )
    d_shift_a = jnp.sum(d_attn_part, axis=1)
    d_scale_a = jnp.sum(d_attn_part * normed_a, axis=1)
    ones = jnp.where(tensor_at == 0, 1.0, 0.0)
    d_modulation = jnp.concatenate(
        [d_shift_a, d_scale_a, d_gate_a * ones, d_shift_f * ones, d_scale_f * ones, d_gate_f],
        axis=1,
    )
    d_attn_own, ffn_own, grads, d_mod_all, d_act = final_sums(
        d_attn_part, ffn_part, grads, d_modulation, w_ada
    )
    grad_attn, grad_ffn = grads[:, : 4 * local], grads[:, 4 * local :]
    first = tensor_at * own_tokens
    own = lambda value: lax.dynamic_slice_in_dim(value, first, own_tokens, 1)
    latent_out = (own(resid) + gate_f * ffn_own).astype(bf16)
    grad_latent = own(d_resid) + norm_back(
        own(normed_a), own(inverse_a), d_attn_own * (1.0 + scale_a)
    )

    grad_ada = dot("ld,le->de", cond_mine, d_mod_all)
    grad_condition = jax.vjp(silu_value, condition.astype(f32))[1](d_act)[0]

    grad_qkv = jnp.stack([grad_attn[:, j * local : (j + 1) * local] for j in range(3)], axis=0)
    grad_proj = grad_attn[:, 3 * local :].T
    grad_up = grad_ffn[:, :units]
    grad_down = grad_ffn[:, units:].T
    return (
        latent_out,
        grad_latent,
        grad_condition,
        grad_ada,
        grad_qkv,
        grad_proj,
        grad_up,
        grad_down,
    )


def solution(mesh):
    return jax.shard_map(
        shards,
        mesh=mesh,
        in_specs=(
            P("dp", "tensor", None),
            P("dp", None),
            P("dp", "tensor"),
            P(None, "dp", "tensor"),
            P("tensor", "dp"),
            P("dp", "tensor"),
            P("tensor", "dp"),
            P("dp", "tensor", None),
        ),
        out_specs=(
            P("dp", "tensor", None),
            P("dp", "tensor", None),
            P("dp", None),
            P("dp", "tensor"),
            P(None, "dp", "tensor"),
            P("tensor", "dp"),
            P("dp", "tensor"),
            P("tensor", "dp"),
        ),
        check_vma=False,
    )
```
